32 devices in a mesh: rows: 8 (over y, x, core), gz: 4 (over z).
Axes of the slice: x: 2, y: 2, z: 4, core: 2. Of those that a mesh axis runs over, the one named last changes fastest.
Arguments:
- segment_warming: float32 [64, 1024, 1024], P('gz', 'rows'), may hold values from 0.15 to 3
- eigenfunction_crosssections: float32 [10, 1024, 1024], P(None, 'rows'), may hold values from -2.5 to 2.5
- segment_phasors: float32 [64, 10], P('gz'), may hold values from 0.2 to 2
- injected_coefficients: float32 [2, 10], replicated, may hold values from -6 to 6
Outputs:
- diffused_warmth: float32 [64, 1024, 1024], P('gz', 'rows')
- refreshed_coupling_sums: float32 [64, 10, 10], P('gz')
- incoming_coefficients: float32 [64, 2, 10], P('gz')
The draws below stay inside these ranges and needn't reach their ends.
All inputs are finite; a program needn't handle non-finite values.
Results may differ from the reference program's by a relative error of at most 0.0003.
Values sent between devices are 32-bit elements; how exact they have to be, the bound alone decides.
A program may use at most 256 MiB of HBM per device.

```python
import math
import jax
import jax.numpy as jnp
from jax import lax

NX = 1024
NY = 1024
M = 10
DIFFUSION_PASSES = 16
Z = 64


def transverse_grid():
    x_coord = (jnp.arange(NX, dtype=jnp.float32) + 0.5) * (2.0 / NX) - 1.0
    y_coord = (jnp.arange(NY, dtype=jnp.float32) + 0.5) * (2.0 / NY) - 1.0
    return (x_coord, y_coord)


def mode_orders(mode_count):
    order_pairs = []
    degree_sum = 0
    while len(order_pairs) < mode_count:
        for x_order in range(degree_sum, -1, -1):
            if len(order_pairs) < mode_count:
                order_pairs.append((x_order, degree_sum - x_order))
        degree_sum += 1
    return order_pairs


def hermite_table(coord, width, degree):
    scaled = coord / width
    polynomials = [jnp.ones_like(scaled), 2.0 * scaled]
    for level in range(1, degree):
        polynomials.append(2.0 * scaled * polynomials[level] - 2.0 * level * polynomials[level - 1])
    envelope = jnp.exp(-0.5 * scaled * scaled)
    return [poly_value * envelope for poly_value in polynomials[:degree + 1]]


def unit_power(shapes):
    return shapes / jnp.sqrt(jnp.mean(shapes * shapes, axis=(1, 2), keepdims=True))


def draw_eigenfunction_crosssections(key, part):
    x_coord, y_coord = transverse_grid()
    width_key = jax.random.fold_in(key, 11)
    mixing_key = jax.random.fold_in(key, 12)
    noise_key = jax.random.fold_in(key, 13)
    widths = jax.random.uniform(width_key, (2,), jnp.float32, 0.6, 0.8)
    strength = 0.35
    noise = 0.1 * jax.random.normal(noise_key, (M, NX, NY), jnp.float32)
    order_pairs = mode_orders(M)
    top_degree = max(1, max((max(order_pair) for order_pair in order_pairs)))
    x_table = hermite_table(x_coord, widths[0], top_degree)
    y_table = hermite_table(y_coord, widths[1], top_degree)
    shapes = jnp.stack([x_table[order_pair[0]][:, None] * y_table[order_pair[1]][None, :] for order_pair in order_pairs])
    shapes = unit_power(shapes)
    mixing = jnp.eye(M, dtype=jnp.float32) + strength * jax.random.normal(mixing_key, (M, M), jnp.float32)
    smooth = unit_power(jnp.einsum('mn,nxy->mxy', mixing, shapes, precision=lax.Precision.HIGHEST))
    noisy = smooth + noise
    peak = jnp.max(jnp.abs(noisy), axis=(1, 2), keepdims=True)
    return (2.5 * noisy / peak).astype(jnp.float32)


def draw_segment_warming(key, part):
    x_coord, y_coord = transverse_grid()
    wave_key = jax.random.fold_in(key, 21)
    phase_key = jax.random.fold_in(key, 22)
    noise_key = jax.random.fold_in(key, 23)
    tilt = 1.0 + 0.4 * x_coord
    strength = 0.5
    noise = jax.random.uniform(noise_key, (Z, NX, NY), jnp.float32, 0.6, 1.4)
    waves = jax.random.uniform(wave_key, (Z, 2), jnp.float32, 0.5, 3.0)
    phases = jax.random.uniform(phase_key, (Z,), jnp.float32, -math.pi, math.pi)
    argument = waves[:, 0, None, None] * x_coord[None, :, None] + waves[:, 1, None, None] * y_coord[None, None, :]
    grating = jnp.cos(math.pi * argument + phases[:, None, None])
    return (tilt[None, :, None] * (1.0 + strength * grating) * noise).astype(jnp.float32)


def level_of(stream_key, shape, pieces, least, largest):
    gain = 1.0
    for dim, shards_of in pieces:
        draws = jax.random.uniform(jax.random.fold_in(jax.random.fold_in(stream_key, 6), dim), (shards_of,), jnp.float32, least / len(pieces), largest / len(pieces))
        gain = gain * jnp.repeat(jnp.exp(draws), shape[dim] // shards_of).reshape((-1,) + (1,) * (len(shape) - 1 - dim))
    return gain


def normal_values(rng, shape, spread, bound, kind=jnp.bfloat16):
    return jnp.clip(spread * jax.random.normal(rng, shape, jnp.float32), -bound, bound).astype(kind)


def setup_inputs(seed: int = 0) -> dict:
    key_of = jax.random.split(jax.random.key(seed), 5)
    return {
        "segment_warming": draw_segment_warming(jax.random.fold_in(key_of[4], 71), 0),
        "eigenfunction_crosssections": draw_eigenfunction_crosssections(jax.random.fold_in(key_of[4], 71), 0),
        "segment_phasors": jnp.clip(jnp.exp(math.log(2.0) - 2.3025851 * jax.random.uniform(key_of[2], (Z, M), jnp.float32) ** level_of(key_of[2], (Z, M), ((0, 4),), -0.2, 0.2)), 0.2, 2.0),
        "injected_coefficients": normal_values(key_of[3], (2, M), 1.0, 6.0, jnp.float32),
    }


highest = lax.Precision.HIGHEST

def factor_entries(matrix):
    count = matrix.shape[-1]
    lower = [[None] * count for index in range(count)]
    for row in range(count):
        for column in range(row + 1):
            total = matrix[..., row, column]
            for inner in range(column):
                total = total - lower[row][inner] * lower[column][inner]
            if row == column:
                lower[row][column] = jnp.sqrt(total)
            else:
                lower[row][column] = total / lower[column][column]
    return lower

def cholesky_solve(lower, rhs):
    count = rhs.shape[-2]
    forward = []
    for row in range(count):
        total = rhs[..., row, :]
        for inner in range(row):
            total = total - lower[row][inner][..., None] * forward[inner]
        forward.append(total / lower[row][row][..., None])
    backward = [None] * count
    for row in range(count - 1, -1, -1):
        total = forward[row]
        for inner in range(row + 1, count):
            total = total - lower[inner][row][..., None] * backward[inner]
        backward[row] = total / lower[row][row][..., None]
    return jnp.stack(backward, axis=-2)

def propagators(constants, intersection_matrix):
    count = intersection_matrix.shape[-1]
    identity = jnp.eye(count, dtype=jnp.float32)
    doubled = intersection_matrix + jnp.swapaxes(intersection_matrix, -1, -2)
    coupled = doubled + identity * constants[..., None]
    squared = jnp.matmul(coupled, coupled, precision=highest)
    lower = factor_entries(identity + squared)
    return (cholesky_solve(lower, identity - squared), cholesky_solve(lower, 2.0 * coupled))

def rotate(matrix_real, matrix_imag, amplitude):
    real_amp = jnp.dot(matrix_real, amplitude[0], precision=highest) - jnp.dot(matrix_imag, amplitude[1], precision=highest)
    imag_amp = jnp.dot(matrix_real, amplitude[1], precision=highest) + jnp.dot(matrix_imag, amplitude[0], precision=highest)
    return jnp.stack([real_amp, imag_amp])

def march(matrices_real, matrices_imag, amplitude):

    def advance_one(carry, pair):
        return (rotate(pair[0], pair[1], carry), carry)
    final_amp, entrances = lax.scan(advance_one, amplitude, (matrices_real, matrices_imag))
    return entrances

def segment_coupling_sums(eigenfunction_crosssections, warmth_distribution):
    count = eigenfunction_crosssections.shape[0]
    flat = eigenfunction_crosssections.reshape(count, -1)
    weighted = (eigenfunction_crosssections * warmth_distribution[None]).reshape(count, -1)
    return jnp.dot(weighted, flat.T, precision=highest) / float(NX * NY)

def heat_source(eigenfunction_crosssections, amplitude):
    count = eigenfunction_crosssections.shape[0]
    flat = eigenfunction_crosssections.reshape(count, -1)
    field = jnp.einsum('zkm,mc->zkc', amplitude, flat, precision=highest)
    intensity = lax.optimization_barrier(jnp.sum(field * field, axis=1))
    return intensity.reshape((amplitude.shape[0],) + eigenfunction_crosssections.shape[1:])

def advance(padded, source):
    side_padded = jnp.pad(padded, ((0, 0), (0, 0), (1, 1)))
    center = side_padded[:, 1:-1, 1:-1]
    laplace = side_padded[:, 2:, 1:-1] + side_padded[:, :-2, 1:-1] + side_padded[:, 1:-1, 2:] + side_padded[:, 1:-1, :-2] - 4.0 * center
    return center + 0.2 * laplace + 0.01 * source

def reference(segment_warming, eigenfunction_crosssections, segment_phasors, injected_coefficients):
    beginning_value = lax.map(lambda warmth_distribution: segment_coupling_sums(eigenfunction_crosssections, warmth_distribution), segment_warming)
    matrices_real, matrices_imag = propagators(segment_phasors, beginning_value * 0.5 * 2.0)
    incoming_coefficients = march(matrices_real, matrices_imag, injected_coefficients)

    def advance_segment(pair):
        warmth_distribution, amplitude = pair
        source = heat_source(eigenfunction_crosssections, amplitude[None])
        field = warmth_distribution[None]
        for subcycle in range(DIFFUSION_PASSES):
            field = advance(jnp.pad(field, ((0, 0), (1, 1), (0, 0))), source)
        return (field[0], segment_coupling_sums(eigenfunction_crosssections, field[0]))
    diffused_warmth, refreshed_coupling_sums = lax.map(advance_segment, (segment_warming, incoming_coefficients))
    return (diffused_warmth, refreshed_coupling_sums, incoming_coefficients)
```

```python
import functools
import math

import jax
import jax.numpy as jnp
import numpy as np
from jax import lax
from jax.experimental import pallas as pl
from jax.experimental.pallas import tpu as pltpu
from jax.sharding import PartitionSpec as P

PASSES = 16
LANES = 128
SUB = 8
MIB = 1024 * 1024
MESH = pl.DeviceIdType.MESH
highest = lax.Precision.HIGHEST


def pair_list(count):
    return [(m, n) for m in range(count) for n in range(m, count)]


def padded(size, unit):
    return -(-size // unit) * unit


def iota(shape, dim):
    return lax.broadcasted_iota(jnp.int32, shape, dim)


def split(value):
    high = value.astype(jnp.bfloat16)
    low = (value - high.astype(jnp.float32)).astype(jnp.bfloat16)
    return high, low


def write_pairs(count, modes, pairs_ref):
    pairs = pair_list(count)
    half = pairs_ref.shape[0] // 2
    for first in range(0, half // SUB, 2):
        products = []
        for pair in range(first, first + 2):
            if pair < len(pairs):
                m, n = pairs[pair]
                products.append(modes(m) * modes(n))
            else:
                products.append(jnp.zeros_like(products[0]))
        high, low = split(jnp.concatenate(products, axis=0))
        at = first * SUB
        pairs_ref[at : at + 2 * SUB] = high
        pairs_ref[half + at : half + at + 2 * SUB] = low


def gram_step(warmth, pairs_ref, warm_ref, total):
    slots = warmth.shape[0]
    high, low = split(warmth)
    warm_ref[:slots] = high
    warm_ref[slots:] = low
    total[...] += lax.dot_general(
        pairs_ref[...],
        warm_ref[...],
        (((1,), (1,)), ((), ())),
        preferred_element_type=jnp.float32,
    )


def gram_finish(total, slices, row_major):
    half = total.shape[0] // 2
    slots = total.shape[1] // 2
    both = (total[half:, slots:] + total[half:, :slots]) + total[:half, slots:] + total[:half, :slots]
    row = iota((half, slots), 0) % SUB
    column = iota((half, slots), 1)
    column_row = column // slices if row_major else column % SUB
    kept = jnp.where(row == column_row, both, 0.0)
    kept = jnp.sum(kept.reshape(half // SUB, SUB, slots), axis=1)
    source = iota((slots, LANES), 0)
    source_slice = source % slices if row_major else source // SUB
    gather = (source_slice == iota((slots, LANES), 1)).astype(jnp.float32)
    return jnp.dot(kept, gather, precision=highest, preferred_element_type=jnp.float32)


def gram_kernel(warm_ref, mode_ref, out_ref, pairs_ref, split_ref, total):
    count = mode_ref.shape[0]
    slices = warm_ref.shape[0]

    @pl.when(pl.program_id(0) == 0)
    def _():
        total[...] = jnp.zeros_like(total)

    write_pairs(count, lambda m: mode_ref[m], pairs_ref)
    gram_step(warm_ref[...].reshape(slices * SUB, warm_ref.shape[2]), pairs_ref, split_ref, total)

    @pl.when(pl.program_id(0) == pl.num_programs(0) - 1)
    def _():
        out_ref[...] = gram_finish(total[...], slices, False)


def gram(warm, modes):
    slices, rows, width = warm.shape
    count = modes.shape[0]
    pair_rows = padded(len(pair_list(count)), 2) * SUB
    return pl.pallas_call(
        gram_kernel,
        grid=(rows // SUB,),
        out_shape=jax.ShapeDtypeStruct((pair_rows // SUB, LANES), jnp.float32),
        in_specs=[
            pl.BlockSpec((slices, SUB, width), lambda i: (0, i, 0)),
            pl.BlockSpec((count, SUB, width), lambda i: (0, i, 0)),
        ],
        out_specs=pl.BlockSpec((pair_rows // SUB, LANES), lambda i: (0, 0)),
        scratch_shapes=[
            pltpu.VMEM((2 * pair_rows, width), jnp.bfloat16),
            pltpu.VMEM((2 * slices * SUB, width), jnp.bfloat16),
            pltpu.VMEM((2 * pair_rows, 2 * slices * SUB), jnp.float32),
        ],
        compiler_params=pltpu.CompilerParams(vmem_limit_bytes=40 * MIB),
        cost_estimate=pl.CostEstimate(flops=20_000_000_000, bytes_accessed=14_000_000, transcendentals=0),
    )(warm, modes)


def share_rows(part_ref, gathered, send_sem, recv_sem, nr):
    me = lax.axis_index("rows")
    copies = []
    for d in range(1, nr):
        copy = pltpu.make_async_remote_copy(
            src_ref=part_ref,
            dst_ref=gathered.at[me],
            send_sem=send_sem.at[d],
            recv_sem=recv_sem.at[d],
            device_id={"rows": lax.rem(me + d, nr)},
            device_id_type=MESH,
        )
        copy.start()
        copies.append(copy)
    gathered[me] = part_ref[...]
    for copy in copies:
        copy.wait()
    total = gathered[0]
    for r in range(1, nr):
        total = total + gathered[r]
    return total


def meet(nr, ng):
    barrier = pltpu.get_barrier_semaphore()
    me = lax.axis_index("rows")
    for d in range(1, nr):
        pl.semaphore_signal(barrier, inc=1, device_id={"rows": lax.rem(me + d, nr)}, device_id_type=MESH)
    gz = lax.axis_index("gz")
    for d in range(1, ng):
        pl.semaphore_signal(barrier, inc=1, device_id={"gz": lax.rem(gz + d, ng)}, device_id_type=MESH)
    pl.semaphore_wait(barrier, nr - 1 + ng - 1)


def spread(row, rows):
    return jnp.broadcast_to(row, (rows, row.shape[1]))


def propagator_kernel(
    nr, ng, count, slices, levels,
    part_ref, phasor_ref, expand_ref, start_ref, out_ref,
    gathered, message, sections, c_ref, x_ref, re_ref, im_ref, late_re, late_im,
    send_sem, recv_sem, send_gz, recv_gz,
):
    meet(nr, ng)
    total = share_rows(part_ref, gathered, send_sem, recv_sem, nr)
    gz = lax.axis_index("gz")
    pairs = part_ref.shape[0]
    message[:pairs] = pltpu.roll(total, gz * slices, 1)
    message[pairs:] = pltpu.roll(phasor_ref[...], gz * slices, 1)
    copies = []
    for d in range(1, ng):
        copy = pltpu.make_async_remote_copy(
            src_ref=message,
            dst_ref=sections.at[gz],
            send_sem=send_gz.at[d],
            recv_sem=recv_gz.at[d],
            device_id={"gz": lax.rem(gz + d, ng)},
            device_id_type=MESH,
        )
        copy.start()
        copies.append(copy)
    sections[gz] = message[...]
    for copy in copies:
        copy.wait()
    every = sections[0]
    for s in range(1, ng):
        every = every + sections[s]
    wide = c_ref.shape[1]
    coupled = jnp.dot(expand_ref[...], every, precision=highest, preferred_element_type=jnp.float32)
    c_ref[...] = coupled.reshape(count, wide, LANES)
    place = iota((wide, LANES), 0)
    unit = [(place == i).astype(jnp.float32) for i in range(count)]
    c = [c_ref[i] for i in range(count)]
    a = []
    for i in range(count):
        acc = unit[i]
        for k in range(count):
            acc = acc + spread(c_ref[i, pl.ds(k, 1), :], wide) * c[k]
        a.append(acc)
    for k in range(count):
        inverse = 1.0 / spread(a[k][k : k + 1], wide)
        pivot = jnp.where(place == k, inverse, a[k] * inverse)
        for i in range(count):
            if i != k:
                factor = spread(a[i][k : k + 1], wide)
                a[i] = jnp.where(place == k, 0.0, a[i]) - factor * pivot
        a[k] = pivot
    for i in range(count):
        x_ref[i] = a[i]
        re_ref[i] = 2.0 * a[i] - unit[i]
    for i in range(count):
        acc = jnp.zeros((wide, LANES), jnp.float32)
        for k in range(count):
            acc = acc + spread(x_ref[i, pl.ds(k, 1), :], wide) * c[k]
        im_ref[i] = 2.0 * acc
    lane = iota((wide, LANES), 1)

    def level(step, carry):
        shift = jnp.left_shift(1, step)
        early_re = [jnp.where(lane < shift, unit[k], pltpu.roll(re_ref[k], shift, 1)) for k in range(count)]
        early_im = [jnp.where(lane < shift, 0.0, pltpu.roll(im_ref[k], shift, 1)) for k in range(count)]
        for i in range(count):
            late_re[i] = re_ref[i]
            late_im[i] = im_ref[i]
        for i in range(count):
            new_re = jnp.zeros((wide, LANES), jnp.float32)
            new_im = jnp.zeros((wide, LANES), jnp.float32)
            for k in range(count):
                fr = spread(late_re[i, pl.ds(k, 1), :], wide)
                fi = spread(late_im[i, pl.ds(k, 1), :], wide)
                new_re = new_re + (fr * early_re[k] - fi * early_im[k])
                new_im = new_im + (fr * early_im[k] + fi * early_re[k])
            re_ref[i] = new_re
            im_ref[i] = new_im
        return carry

    lax.fori_loop(0, levels, level, 0)
    start_re = start_ref[0]
    start_im = start_ref[1]
    out_ref[...] = jnp.zeros_like(out_ref)
    for i in range(count):
        er = jnp.where(lane < 1, unit[i], pltpu.roll(re_ref[i], 1, 1))
        ei = jnp.where(lane < 1, 0.0, pltpu.roll(im_ref[i], 1, 1))
        amp_re = jnp.sum(er * start_re - ei * start_im, axis=0, keepdims=True)
        amp_im = jnp.sum(er * start_im + ei * start_re, axis=0, keepdims=True)
        out_ref[0, pl.ds(i, 1), :] = amp_re
        out_ref[1, pl.ds(i, 1), :] = amp_im


def expansion(count, wide, extra, scale):
    pairs = pair_list(count)
    rows = padded(len(pairs), 2)
    table = np.zeros((count * wide, rows + extra), np.float32)
    for index, (m, n) in enumerate(pairs):
        table[m * wide + n, index] = scale
        table[n * wide + m, index] = scale
    if extra:
        for m in range(count):
            table[m * wide + m, rows + m] = 1.0
    return table


def amplitudes(nr, ng, part, phasors, start, cells):
    slices, count = phasors.shape
    wide = padded(count, SUB)
    pairs = part.shape[0]
    expand = jnp.asarray(expansion(count, wide, wide, 2.0 / cells))
    phasor = jnp.pad(phasors.T, ((0, wide - count), (0, LANES - slices)))
    begin = jnp.broadcast_to(jnp.pad(start, ((0, 0), (0, wide - count)))[:, :, None], (2, wide, LANES))
    vmem = pl.BlockSpec(memory_space=pltpu.VMEM)
    matrix = pltpu.VMEM((count, wide, LANES), jnp.float32)
    levels = max(1, math.ceil(math.log2(slices * ng)))
    return pl.pallas_call(
        functools.partial(propagator_kernel, nr, ng, count, slices, levels),
        out_shape=jax.ShapeDtypeStruct((2, wide, LANES), jnp.float32),
        in_specs=[vmem] * 4,
        out_specs=vmem,
        scratch_shapes=[
            pltpu.VMEM((nr, pairs, LANES), jnp.float32),
            pltpu.VMEM((pairs + wide, LANES), jnp.float32),
            pltpu.VMEM((ng, pairs + wide, LANES), jnp.float32),
            matrix, matrix, matrix, matrix, matrix, matrix,
            pltpu.SemaphoreType.DMA((nr,)),
            pltpu.SemaphoreType.DMA((nr,)),
            pltpu.SemaphoreType.DMA((ng,)),
            pltpu.SemaphoreType.DMA((ng,)),
        ],
        compiler_params=pltpu.CompilerParams(collective_id=1, has_side_effects=True),
        cost_estimate=pl.CostEstimate(flops=20_000_000_000, bytes_accessed=200_000, transcendentals=0),
    )(part, phasor, expand, begin)


def final_kernel(nr, part_ref, expand_ref, out_ref, gathered, send_sem, recv_sem):
    meet(nr, 1)
    total = share_rows(part_ref, gathered, send_sem, recv_sem, nr)
    out_ref[...] = jnp.dot(expand_ref[...], total, precision=highest, preferred_element_type=jnp.float32)


def final_sums(nr, part, count, slices, cells):
    wide = padded(count, SUB)
    expand = jnp.asarray(expansion(count, wide, 0, 1.0 / cells))
    vmem = pl.BlockSpec(memory_space=pltpu.VMEM)
    out = pl.pallas_call(
        functools.partial(final_kernel, nr),
        out_shape=jax.ShapeDtypeStruct((count * wide, LANES), jnp.float32),
        in_specs=[vmem] * 2,
        out_specs=vmem,
        scratch_shapes=[
            pltpu.VMEM((nr,) + part.shape, jnp.float32),
            pltpu.SemaphoreType.DMA((nr,)),
            pltpu.SemaphoreType.DMA((nr,)),
        ],
        compiler_params=pltpu.CompilerParams(collective_id=2, has_side_effects=True),
    )(part, expand)
    return jnp.transpose(out.reshape(count, wide, LANES)[:, :count, :slices], (2, 0, 1))


def heat_kernel(
    nr,
    warm_hbm, low_hbm, high_hbm, mode_hbm, mode_low, mode_high, amp_ref,
    out_hbm, part_ref,
    natural, modes, first, second, source, pairs_ref, split_ref, total, stack_ref, lhs_ref,
    sems, out_sems,
):
    slices, rows, width = warm_hbm.shape
    count = mode_hbm.shape[0]
    halo = low_hbm.shape[1]
    tall = rows + 2 * halo
    tiles = tall // SUB
    me = lax.axis_index("rows")
    loads = [
        pltpu.make_async_copy(mode_low, modes.at[:, pl.ds(0, halo)], sems.at[0]),
        pltpu.make_async_copy(mode_hbm, modes.at[:, pl.ds(halo, rows)], sems.at[1]),
        pltpu.make_async_copy(mode_high, modes.at[:, pl.ds(halo + rows, halo)], sems.at[2]),
        pltpu.make_async_copy(low_hbm, natural.at[:, pl.ds(0, halo)], sems.at[3]),
        pltpu.make_async_copy(warm_hbm, natural.at[:, pl.ds(halo, rows)], sems.at[4]),
        pltpu.make_async_copy(high_hbm, natural.at[:, pl.ds(halo + rows, halo)], sems.at[5]),
    ]
    for load in loads:
        load.start()
    depth = stack_ref.shape[0]
    seg = count * SUB
    column = iota((amp_ref.shape[1], depth), 1)
    pick = ((column % seg) // SUB == iota((amp_ref.shape[1], depth), 0)) & (column < 3 * seg)
    wave = jnp.dot(0.1 * amp_ref[...], pick.astype(jnp.float32), precision=highest, preferred_element_type=jnp.float32)
    high = wave.astype(jnp.bfloat16).astype(jnp.float32)
    low = wave - high
    block = wave.shape[0]
    part = jnp.where(iota(wave.shape, 1) < 2 * seg, high, low)
    for r in range(SUB):
        lhs_ref[r * block : (r + 1) * block] = jnp.where(iota(wave.shape, 1) % SUB == r, part, 0.0).astype(jnp.bfloat16)
    stack_ref[...] = jnp.zeros_like(stack_ref)
    for load in loads[:3]:
        load.wait()

    def source_tile(t, carry):
        at = pl.ds(pl.multiple_of(t * SUB, SUB), SUB)
        tile = modes[:, at, :].reshape(seg, width)
        hi, lo = split(tile)
        stack_ref[:seg] = hi
        stack_ref[seg : 2 * seg] = lo
        stack_ref[2 * seg : 3 * seg] = hi
        for r in range(SUB):
            waves = jnp.dot(
                lhs_ref[r * block : (r + 1) * block], stack_ref[...], preferred_element_type=jnp.float32
            )
            re, im = waves[:slices], waves[slices:]
            source[t * SUB + r] = re * re + im * im
        return carry

    lax.fori_loop(0, tiles, source_tile, 0)
    for load in loads[3:]:
        load.wait()

    def to_rows(t, carry):
        at = pl.ds(pl.multiple_of(t * SUB, SUB), SUB)
        for c in range(0, width, LANES):
            first[at, :, c : c + LANES] = jnp.swapaxes(natural[:, at, c : c + LANES], 0, 1)
        return carry

    lax.fori_loop(0, tiles, to_rows, 0)
    second[0] = jnp.zeros_like(second[0])
    second[tall - 1] = jnp.zeros_like(second[0])
    lane = iota((1, slices, LANES), 2)
    at_first = lane == 0
    at_last = lane == LANES - 1
    bottom = jnp.where(me == 0, halo, 0)
    top = jnp.where(me == nr - 1, halo + rows, tall)

    def subcycle(src, dst, lowest, highest_row):
        group = 2

        def rows_at(g, carry):
            r = lowest + g * group
            factors = [jnp.where((r + i >= bottom) & (r + i < top), 0.2, 0.0).astype(jnp.float32) for i in range(group)]
            zero = jnp.zeros((1, slices, LANES), jnp.float32)
            columns = width // LANES

            def rolled(i, c):
                if 0 <= c < columns:
                    v = src[pl.ds(r + i, 1), :, c * LANES : (c + 1) * LANES]
                    return v, pltpu.roll(v, 1, 2), pltpu.roll(v, LANES - 1, 2)
                return zero, zero, zero

            for i in range(group):
                before = rolled(i, -1)
                here = rolled(i, 0)
                for c in range(columns):
                    after = rolled(i, c + 1)
                    lanes = slice(c * LANES, (c + 1) * LANES)
                    west = jnp.where(at_first, before[1], here[1])
                    east = jnp.where(at_last, after[2], here[2])
                    north = src[pl.ds(r + i - 1, 1), :, lanes]
                    south = src[pl.ds(r + i + 1, 1), :, lanes]
                    five = (here[0] + (north + south)) + (west + east)
                    dst[pl.ds(r + i, 1), :, lanes] = factors[i] * five + source[pl.ds(r + i, 1), :, lanes]
                    before, here = here, after
            return carry

        lax.fori_loop(0, (highest_row - lowest) // group, rows_at, 0)

    for p in range(0, PASSES, 2):
        subcycle(first, second, p + 1, tall - 1 - p)
        subcycle(second, first, p + 2, tall - 2 - p)

    total[...] = jnp.zeros_like(total)
    writes = pltpu.make_async_copy(natural.at[:, pl.ds(halo, rows)], out_hbm, out_sems.at[0])

    def from_rows(t, carry):
        at = pl.ds(pl.multiple_of(halo + t * SUB, SUB), SUB)
        for c in range(0, width, LANES):
            natural[:, at, c : c + LANES] = jnp.swapaxes(first[at, :, c : c + LANES], 0, 1)
        return carry

    lax.fori_loop(0, rows // SUB, from_rows, 0)
    writes.start()

    def sums(t, carry):
        at = pl.ds(pl.multiple_of(halo + t * SUB, SUB), SUB)
        write_pairs(count, lambda m: modes[m, at, :], pairs_ref)
        gram_step(first[at].reshape(SUB * slices, width), pairs_ref, split_ref, total)
        return carry

    lax.fori_loop(0, rows // SUB, sums, 0)
    part_ref[...] = gram_finish(total[...], slices, True)
    writes.wait()


def heat(nr, warm, low, high, modes, mode_low, mode_high, amp):
    slices, rows, width = warm.shape
    count = modes.shape[0]
    halo = low.shape[1]
    tall = rows + 2 * halo
    pair_rows = padded(len(pair_list(count)), 2) * SUB
    anywhere = pl.BlockSpec(memory_space=pltpu.HBM)
    vmem = pl.BlockSpec(memory_space=pltpu.VMEM)
    depth = padded(3 * count * SUB, LANES)
    by_row = pltpu.VMEM((tall, slices, width), jnp.float32)
    return pl.pallas_call(
        functools.partial(heat_kernel, nr),
        out_shape=(
            jax.ShapeDtypeStruct(warm.shape, jnp.float32),
            jax.ShapeDtypeStruct((pair_rows // SUB, LANES), jnp.float32),
        ),
        in_specs=[anywhere] * 6 + [vmem],
        out_specs=(anywhere, vmem),
        scratch_shapes=[
            pltpu.VMEM((slices, tall, width), jnp.float32),
            pltpu.VMEM((count, tall, width), jnp.float32),
            by_row, by_row, by_row,
            pltpu.VMEM((2 * pair_rows, width), jnp.bfloat16),
            pltpu.VMEM((2 * slices * SUB, width), jnp.bfloat16),
            pltpu.VMEM((2 * pair_rows, 2 * slices * SUB), jnp.float32),
            pltpu.VMEM((depth, width), jnp.bfloat16),
            pltpu.VMEM((SUB * 2 * slices, depth), jnp.bfloat16),
            pltpu.SemaphoreType.DMA((6,)),
            pltpu.SemaphoreType.DMA((1,)),
        ],
        compiler_params=pltpu.CompilerParams(vmem_limit_bytes=63 * MIB),
    )(warm, low, high, modes, mode_low, mode_high, amp)


def with_neighbours(block, width):
    count = lax.axis_size("rows")
    forward = [(i, i + 1) for i in range(count - 1)]
    backward = [(i + 1, i) for i in range(count - 1)]
    rows = block.shape[1]
    low = lax.ppermute(lax.slice_in_dim(block, rows - width, None, axis=1), "rows", forward)
    high = lax.ppermute(lax.slice_in_dim(block, 0, width, axis=1), "rows", backward)
    return low, high


def shards(cells, warm, modes, phasors, start):
    nr = lax.axis_size("rows")
    ng = lax.axis_size("gz")
    slices = warm.shape[0]
    count = modes.shape[0]
    mode_low, mode_high = with_neighbours(modes, PASSES)
    low, high = with_neighbours(warm, PASSES)
    part = gram(warm, modes)
    amp = amplitudes(nr, ng, part, phasors, start, cells)
    local = lax.dynamic_slice_in_dim(amp, lax.axis_index("gz") * slices, slices, axis=2)
    incoming = jnp.transpose(local, (2, 0, 1))[:, :, :count]
    by_part = jnp.transpose(local, (0, 2, 1)).reshape(2 * slices, local.shape[1])
    heated, new_part = heat(nr, warm, low, high, modes, mode_low, mode_high, by_part)
    sums = final_sums(nr, new_part, count, slices, cells)
    return heated, sums, incoming


def solution(mesh):
    placed = (P("gz", "rows", None), P(None, "rows", None), P("gz", None), P())

    def whole(warm, modes, phasors, start):
        cells = warm.shape[1] * warm.shape[2]
        return jax.shard_map(
            functools.partial(shards, cells),
            mesh=mesh,
            in_specs=placed,
            out_specs=(P("gz", "rows", None), P("gz", None, None), P("gz", None, None)),
            check_vma=False,
        )(warm, modes, phasors, start)

    return whole
```
